32 devices in a mesh: inner: 4 (over y, x), outer: 8 (over z, core).
Axes of the slice: x: 2, y: 2, z: 4, core: 2. Of those that a mesh axis runs over, the one named last changes fastest.
Arguments:
- jac: float32 [512, 256, 256], P(('outer', 'inner')), may hold values from -0.5 to 1
- obs: float32 [512, 256], P(('outer', 'inner')), may hold values from -6 to 6
- gain_filter: float32 [256], replicated, may hold values from 0 to 0.1
- gain_smooth: float32 [256, 256], replicated, may hold values from -0.5 to 1
- init_mean: float32 [256], replicated, may hold values from -6 to 6
Outputs:
- filtered: float32 [512, 256], P(('outer', 'inner'))
- smoothed: float32 [512, 256], P(('outer', 'inner'))
The draws below stay inside these ranges and needn't reach their ends.
All inputs are finite; a program needn't handle non-finite values.
Results may differ from the reference program's by a relative error of at most 0.0003.
Values sent between devices are 32-bit elements; how exact they have to be, the bound alone decides.
A program may use at most 64 MiB of HBM per device.

```python
import math
import jax
import jax.numpy as jnp
from jax import lax

N = 256
TSTEPS = 512


def channel_rates(seed_key, share):
    keys = jax.random.split(jax.random.fold_in(seed_key, 7), 5)
    slow_mask = jax.random.uniform(keys[0], (N,), jnp.float32) < share
    slow_decay = jax.random.uniform(keys[1], (N,), jnp.float32, 0.1, 1.0) / TSTEPS
    fast_decay = jnp.exp(jax.random.uniform(keys[2], (N,), jnp.float32, math.log(0.01), math.log(0.05)))
    slow_gain = jax.random.uniform(keys[3], (N,), jnp.float32, 0.05, 0.5) / TSTEPS
    fast_gain = jnp.exp(jax.random.uniform(keys[4], (N,), jnp.float32, math.log(0.01), math.log(0.1)))
    return (jnp.where(slow_mask, slow_decay, fast_decay), jnp.where(slow_mask, slow_gain, fast_gain))


def draw_jac(key, part):
    share = 0.5
    decay, unused_gain = channel_rates(key, share)
    keys = jax.random.split(jax.random.fold_in(key, 11), 3)
    rough = jnp.exp(jax.random.uniform(keys[0], (TSTEPS, N), jnp.float32, math.log(0.5), math.log(2.0)))
    spots = jax.random.randint(keys[1], (4,), 0, TSTEPS)
    hits = jnp.any(jnp.arange(TSTEPS)[:, None] == spots[None, :], axis=1)
    diagonal = (1.0 - decay[None, :] * rough) * jnp.where(hits, 0.75, 1.0)[:, None]
    noise = jax.random.normal(keys[2], (TSTEPS, N, N), jnp.float32) * (0.015 / math.sqrt(2.0 * N))
    skewed = noise - jnp.swapaxes(noise, 1, 2)
    result = skewed + diagonal[:, :, None] * jnp.eye(N, dtype=jnp.float32)[None]
    return result.astype(jnp.float32)


def draw_gain_filter(key, part):
    share = 0.5
    unused_decay, gains = channel_rates(key, share)
    return gains.astype(jnp.float32)


def draw_gain_smooth(key, part):
    share = 0.5
    decay, unused_gain = channel_rates(key, share)
    keys = jax.random.split(jax.random.fold_in(key, 17), 2)
    rough = jnp.exp(jax.random.uniform(keys[0], (N,), jnp.float32, math.log(0.5), math.log(2.0)))
    noise = jax.random.normal(keys[1], (N, N), jnp.float32) * (0.01 / math.sqrt(2.0 * N))
    skewed = noise - noise.T
    result = skewed + jnp.diag(1.0 - decay * rough)
    return result.astype(jnp.float32)


def level_of(rng, dims, pieces, least, top_value):
    factor_of = 1.0
    for position, parts in pieces:
        heights = jax.random.uniform(jax.random.fold_in(jax.random.fold_in(rng, 6), position), (parts,), jnp.float32, least / len(pieces), top_value / len(pieces))
        factor_of = factor_of * jnp.repeat(jnp.exp(heights), dims[position] // parts).reshape((-1,) + (1,) * (len(dims) - 1 - position))
    return factor_of


def scatter_about(own_key, shape, deviation, bound, pieces=(), held_as=jnp.bfloat16):
    entries = deviation * jax.random.normal(own_key, shape, jnp.float32)
    if pieces:
        entries = entries * level_of(own_key, shape, pieces, -0.22, 0.18)
    return jnp.clip(entries, -bound, bound).astype(held_as)


def setup_inputs(seed: int = 0) -> dict:
    seeds = jax.random.split(jax.random.key(seed), 6)
    return {
        "jac": draw_jac(jax.random.fold_in(seeds[5], 71), 0),
        "obs": scatter_about(seeds[1], (TSTEPS, N), 1.0, 6.0, ((0, 32),), jnp.float32),
        "gain_filter": draw_gain_filter(jax.random.fold_in(seeds[5], 71), 0),
        "gain_smooth": draw_gain_smooth(jax.random.fold_in(seeds[5], 71), 0),
        "init_mean": scatter_about(seeds[4], (N,), 1.0, 6.0, (), jnp.float32),
    }


def reference(jac, obs, gain_filter, gain_smooth, init_mean):
    highest = lax.Precision.HIGHEST

    def forward(state, inputs):
        step_matrix, measured = inputs
        predicted = jnp.dot(step_matrix, state, precision=highest)
        updated = predicted + gain_filter * (measured - predicted)
        return updated, (predicted, updated)

    _, (predicted_all, filtered_all) = lax.scan(forward, init_mean, (jac, obs))

    def backward(state, correction):
        renewed = jnp.dot(gain_smooth, state, precision=highest) + correction
        return renewed, renewed

    _, back_states = lax.scan(backward, jnp.zeros((N,), jnp.float32), filtered_all - predicted_all, reverse=True)
    return filtered_all, predicted_all + back_states
```

```python
import functools

import jax
import jax.numpy as jnp
from jax import lax
from jax.experimental import pallas as pl
from jax.experimental.pallas import tpu as pltpu
from jax.sharding import PartitionSpec as P

F32 = jnp.float32
BF16 = jnp.bfloat16
MESH = pl.DeviceIdType.MESH


def log2(count):
    assert count & (count - 1) == 0
    return count.bit_length() - 1


def split(x):
    high = x.astype(BF16)
    return high, (x - high.astype(F32)).astype(BF16)


def matmul(a, b):
    dot = functools.partial(jnp.dot, preferred_element_type=F32)
    return dot(a[0], b[0]) + (dot(a[0], b[1]) + dot(a[1], b[0]))


def rows_dot(x, matrix):
    rows = x.shape[0]
    high = x.astype(BF16).astype(F32)
    both = jnp.concatenate([high, x - high], 0).astype(BF16)
    dims = (((1,), (1,)), ((), ()))
    out = lax.dot_general(both, matrix[0], dims, preferred_element_type=F32)
    out = out + lax.dot_general(both, matrix[1], dims, preferred_element_type=F32)
    return out[:rows] + out[rows:]


def kernel(
    inner, outer, block,
    jac_ref, obs_ref, gain_ref, smooth_ref, init_ref,
    filtered_ref, smoothed_ref,
    node_hi, node_lo, power_hi, power_lo, left_hi, left_lo, whole_hi, whole_lo,
    mat_out, mat_in, vec_out, vec_in, down_out, down_in, chain_out, chain_in,
    state_ref, pred_ref, own_ref, gather_ref,
    mat_send, mat_recv, vec_send, vec_recv, down_send, down_recv,
    chain_send, chain_recv, gather_send, gather_recv,
):
    steps, width = obs_ref.shape
    devices = inner * outer
    levels = log2(block)
    me = lax.axis_index("outer") * inner + lax.axis_index("inner")

    def place(device):
        return {"outer": device // inner, "inner": lax.rem(device, inner)}

    def remote(src, dst, send, recv, device):
        return pltpu.make_async_remote_copy(
            src_ref=src, dst_ref=dst, send_sem=send, recv_sem=recv,
            device_id=place(device), device_id_type=MESH,
        )

    gather_ref[...] = jnp.zeros_like(gather_ref)
    barrier = pltpu.get_barrier_semaphore()

    def greet(k, _):
        pl.semaphore_signal(
            barrier, inc=1, device_id=place(lax.rem(me + k, devices)), device_id_type=MESH
        )
        return 0

    lax.fori_loop(1, devices, greet, 0)

    def rep(row):
        return jnp.broadcast_to(row, (8, width))

    def node(i):
        return node_hi[i], node_lo[i]

    def put(hi_ref, lo_ref, i, value):
        hi_ref[i], lo_ref[i] = split(value)

    def power(k):
        return power_hi[k], power_lo[k]

    gain = gain_ref[...]
    retain = 1.0 - gain
    shift = obs_ref[...] * (gain / retain)
    for t in range(steps):
        put(node_hi, node_lo, steps + t, jac_ref[t] * retain)
    for i in range(steps - 1, 0, -1):
        product = matmul(node(2 * i + 1), node(2 * i))
        if i > 1:
            put(node_hi, node_lo, i, product)
        else:
            mat_out[0] = product
            put(node_hi, node_lo, 1, product)

    pl.semaphore_wait(barrier, devices - 1)

    def sends(level):
        span = 2 << level
        return lax.rem(me, span) == span // 2 - 1

    def takes(level):
        span = 2 << level
        return lax.rem(me, span) == span - 1

    def mat_copy(level):
        return remote(
            mat_out.at[level], mat_in.at[level], mat_send.at[level], mat_recv.at[level],
            lax.rem(me + (1 << level), devices),
        )

    def vec_copy(level):
        return remote(
            vec_out.at[level], vec_in.at[level], vec_send.at[level], vec_recv.at[level],
            lax.rem(me + (1 << level), devices),
        )

    @pl.when(sends(0))
    def _():
        mat_copy(0).start()

    offset = {steps + t: rep(shift[t : t + 1]) for t in range(steps)}
    for i in range(steps - 1, 0, -1):
        offset[i] = rows_dot(offset[2 * i], node(2 * i + 1)) + offset[2 * i + 1]
    vec_out[0] = offset[1][:1]

    @pl.when(sends(0))
    def _():
        vec_copy(0).start()

    powers = power_hi.shape[0]
    put(power_hi, power_lo, 0, smooth_ref[...])
    for k in range(1, powers):
        put(power_hi, power_lo, k, matmul(power(k - 1), power(k - 1)))

    for level in range(levels):
        @pl.when(takes(level))
        def _():
            mat_copy(level).wait_recv()
            vec_copy(level).wait_recv()
            own = split(mat_out[level])
            put(left_hi, left_lo, level, mat_in[level])
            product = matmul(own, (left_hi[level], left_lo[level]))
            total = rows_dot(rep(vec_in[level]), own) + vec_out[level]
            if level + 1 < levels:
                mat_out[level + 1] = product
            put(whole_hi, whole_lo, 0, product)
            vec_out[level + 1] = total[:1]

        if level + 1 < levels:
            @pl.when(sends(level + 1))
            def _():
                mat_copy(level + 1).start()
                vec_copy(level + 1).start()

    ends = lax.rem(me, block) == block - 1
    chain = remote(
        chain_out, chain_in, chain_send, chain_recv, lax.rem(me + block, devices)
    )

    @pl.when(jnp.logical_and(ends, me < block))
    def _():
        state_ref[...] = init_ref[...] / retain

    @pl.when(jnp.logical_and(ends, me >= block))
    def _():
        chain.wait_recv()
        state_ref[...] = chain_in[...]

    @pl.when(jnp.logical_and(ends, me < devices - block))
    def _():
        after = rows_dot(rep(state_ref[...]), (whole_hi[0], whole_lo[0]))
        chain_out[...] = after[:1] + vec_out[levels]
        chain.start()

    for level in range(levels - 1, -1, -1):
        down = remote(
            down_out.at[level], down_in.at[level], down_send.at[level], down_recv.at[level],
            lax.rem(me + devices - (1 << level), devices),
        )

        @pl.when(takes(level))
        def _():
            down_out[level] = state_ref[...]
            down.start()
            moved = rows_dot(rep(state_ref[...]), (left_hi[level], left_lo[level]))
            state_ref[...] = moved[:1] + vec_in[level]

        @pl.when(sends(level))
        def _():
            down.wait_recv()
            state_ref[...] = down_in[level]

    state = {1: rep(state_ref[...])}
    for i in range(1, steps):
        state[2 * i] = state[i]
        moved = rows_dot(state[i], node(2 * i))
        state[2 * i + 1] = moved + offset[2 * i]
        if 2 * i >= steps:
            t = 2 * i - steps
            pred_ref[t : t + 1] = moved[:1]
            after = rows_dot(state[2 * i + 1], node(2 * i + 1))
            pred_ref[t + 1 : t + 2] = after[:1]

    pred = pred_ref[...]
    filtered = pred + gain * (obs_ref[...] - pred)
    filtered_ref[...] = filtered
    correction = filtered - pred

    def fold(x, first):
        half = x.shape[0] // 2
        while half >= 1:
            step = power(first + log2(half))
            if half >= 8:
                x = x[:half] + rows_dot(x[half:], step)
            else:
                x = x + rows_dot(pltpu.roll(x, 8 - half, 0), step)
            half //= 2
        return x[:1]

    own_ref[...] = fold(correction, 0)

    def gather_copy(k, device):
        return remote(
            own_ref, gather_ref.at[k - 1], gather_send.at[k - 1], gather_recv.at[k - 1], device
        )

    def give(k, _):
        gather_copy(k, me - k).start()
        return 0

    lax.fori_loop(1, me + 1, give, 0)

    def get(k, _):
        gather_copy(k, lax.rem(me + devices - k, devices)).wait_recv()
        return 0

    lax.fori_loop(1, devices - me, get, 0)
    after = fold(gather_ref[:, 0, :], log2(steps))

    row = lax.broadcasted_iota(jnp.int32, (steps, width), 0)
    entering = rows_dot(rep(after), power(0))
    back = correction + jnp.where(row == steps - 1, entering[:1], 0.0)
    reach = 1
    while reach < steps:
        moved = jnp.where(row < steps - reach, pltpu.roll(back, steps - reach, 0), 0.0)
        back = back + rows_dot(moved, power(log2(reach)))
        reach *= 2
    smoothed_ref[...] = pred + back

    def gave(k, _):
        gather_copy(k, me - k).wait_send()
        return 0

    lax.fori_loop(1, me + 1, gave, 0)

    @pl.when(jnp.logical_and(ends, me < devices - block))
    def _():
        chain.wait_send()

    for level in range(levels):
        @pl.when(sends(level))
        def _():
            mat_copy(level).wait_send()
            vec_copy(level).wait_send()

        @pl.when(takes(level))
        def _():
            remote(
                down_out.at[level], down_in.at[level], down_send.at[level], down_recv.at[level],
                lax.rem(me + devices - (1 << level), devices),
            ).wait_send()


def solution(mesh):
    inner, outer = mesh.shape["inner"], mesh.shape["outer"]
    devices = inner * outer
    block = 2 * inner if outer % 2 == 0 else inner
    levels = log2(block)

    def shards(jac, obs, gain_filter, gain_smooth, init_mean):
        steps, width = obs.shape
        powers = log2(steps) + log2(devices)
        square = (width, width)
        vec = (1, width)
        dma = pltpu.SemaphoreType.DMA
        return pl.pallas_call(
            functools.partial(kernel, inner, outer, block),
            out_shape=[jax.ShapeDtypeStruct((steps, width), F32)] * 2,
            in_specs=[pl.BlockSpec(memory_space=pltpu.VMEM)] * 5,
            out_specs=[pl.BlockSpec(memory_space=pltpu.VMEM)] * 2,
            scratch_shapes=[
                pltpu.VMEM((2 * steps, *square), BF16),
                pltpu.VMEM((2 * steps, *square), BF16),
                pltpu.VMEM((powers, *square), BF16),
                pltpu.VMEM((powers, *square), BF16),
                pltpu.VMEM((levels, *square), BF16),
                pltpu.VMEM((levels, *square), BF16),
                pltpu.VMEM((1, *square), BF16),
                pltpu.VMEM((1, *square), BF16),
                pltpu.VMEM((levels, *square), F32),
                pltpu.VMEM((levels, *square), F32),
                pltpu.VMEM((levels + 1, *vec), F32),
                pltpu.VMEM((levels, *vec), F32),
                pltpu.VMEM((levels, *vec), F32),
                pltpu.VMEM((levels, *vec), F32),
                pltpu.VMEM(vec, F32),
                pltpu.VMEM(vec, F32),
                pltpu.VMEM(vec, F32),
                pltpu.VMEM((steps, width), F32),
                pltpu.VMEM(vec, F32),
                pltpu.VMEM((devices, *vec), F32),
                dma((levels,)), dma((levels,)), dma((levels,)), dma((levels,)),
                dma((levels,)), dma((levels,)), dma, dma,
                dma((devices,)), dma((devices,)),
            ],
            compiler_params=pltpu.CompilerParams(
                collective_id=0, has_side_effects=True, vmem_limit_bytes=48 * 2**20
            ),
        )(jac, obs, gain_filter[None], gain_smooth, init_mean[None])

    return jax.shard_map(
        shards,
        mesh=mesh,
        in_specs=(P(("outer", "inner"), None, None), P(("outer", "inner"), None), P(), P(), P()),
        out_specs=(P(("outer", "inner"), None), P(("outer", "inner"), None)),
        check_vma=False,
    )
```

```python
import functools

import jax
import jax.numpy as jnp
from jax import lax
from jax.experimental import pallas as pl
from jax.experimental.pallas import tpu as pltpu
from jax.sharding import PartitionSpec as P

F32 = jnp.float32
BF16 = jnp.bfloat16
MESH = pl.DeviceIdType.MESH


def log2(count):
    assert count & (count - 1) == 0
    return count.bit_length() - 1


def split(x):
    high = x.astype(BF16)
    return high, (x - high.astype(F32)).astype(BF16)


def split3(x):
    high = x.astype(BF16)
    rest = x - high.astype(F32)
    middle = rest.astype(BF16)
    return high, middle, (rest - middle.astype(F32)).astype(BF16)


def matmul(a, b, turned=False):
    dims = (((1,), (1 if turned else 0,)), ((), ()))

    def dot(i, j):
        return lax.dot_general(a[i], b[j], dims, preferred_element_type=F32)

    total = dot(0, 1) + dot(1, 0)
    if len(a) == 3:
        total = total + (dot(1, 1) + (dot(0, 2) + dot(2, 0)))
    return dot(0, 0) + total


def rows_dot(x, matrix, turned=True):
    rows = x.shape[0]
    high = x.astype(BF16).astype(F32)
    both = jnp.concatenate([high, x - high], 0).astype(BF16)
    dims = (((1,), (1 if turned else 0,)), ((), ()))
    out = lax.dot_general(both, matrix[0], dims, preferred_element_type=F32)
    out = out + lax.dot_general(both, matrix[1], dims, preferred_element_type=F32)
    return out[:rows] + out[rows:]


def kernel(
    inner, outer, block, chunks,
    jac_ref, obs_ref, gain_ref, smooth_ref, init_ref,
    filtered_ref, smoothed_ref,
    node_hi, node_lo, node_end, turned_ref, power_hi, power_lo, power_end,
    left_hi, left_lo, whole_hi, whole_lo,
    mat_out, mat_in, vec_out, vec_in, down_out, down_in, chain_out, chain_in,
    state_ref, pred_ref, own_ref, gather_ref,
    mat_send, mat_recv, vec_send, vec_recv, down_send, down_recv,
    chain_send, chain_recv, gather_send, gather_recv,
):
    steps, width = obs_ref.shape
    devices = inner * outer
    levels = log2(block)
    me = lax.axis_index("outer") * inner + lax.axis_index("inner")

    def place(device):
        return {"outer": device // inner, "inner": lax.rem(device, inner)}

    def remote(src, dst, send, recv, device):
        return pltpu.make_async_remote_copy(
            src_ref=src, dst_ref=dst, send_sem=send, recv_sem=recv,
            device_id=place(device), device_id_type=MESH,
        )

    gather_ref[...] = jnp.zeros_like(gather_ref)
    barrier = pltpu.get_barrier_semaphore()

    def greet(k, _):
        pl.semaphore_signal(
            barrier, inc=1, device_id=place(lax.rem(me + k, devices)), device_id_type=MESH
        )
        return 0

    lax.fori_loop(1, devices, greet, 0)

    def rep(row):
        return jnp.broadcast_to(row, (8, width))

    def node(i):
        return node_hi[i], node_lo[i]

    def node3(i):
        return node_hi[i], node_lo[i], node_end[i]

    def put_node(i, value):
        node_hi[i], node_lo[i], node_end[i] = split3(value)

    def power(k):
        return power_hi[k], power_lo[k]

    gain = gain_ref[...]
    retain = 1.0 - gain
    shift = obs_ref[...] * (gain / retain)
    for t in range(steps):
        put_node(steps + t, jac_ref[t] * retain)
    for i in range(steps - 1, 1, -1):
        put_node(i, matmul(node3(2 * i + 1), node3(2 * i)))
    grid = (width, width)
    eye = lax.broadcasted_iota(jnp.int32, grid, 0) == lax.broadcasted_iota(jnp.int32, grid, 1)
    eye = jnp.where(eye, 1.0, 0.0).astype(BF16)
    for k, piece in enumerate(node3(2)):
        turned = lax.dot_general(eye, piece, (((1,), (1,)), ((), ())), preferred_element_type=F32)
        turned_ref[k] = turned.astype(BF16)

    pl.semaphore_wait(barrier, devices - 1)

    def sends(level):
        span = 2 << level
        return lax.rem(me, span) == span // 2 - 1

    def takes(level):
        span = 2 << level
        return lax.rem(me, span) == span - 1

    chunk = width // chunks

    def mat_copy(level, part):
        rows = pl.ds(part * chunk, chunk)
        return remote(
            mat_out.at[level, rows], mat_in.at[level, rows],
            mat_send.at[level, part], mat_recv.at[level, part],
            lax.rem(me + (1 << level), devices),
        )

    def vec_copy(level):
        return remote(
            vec_out.at[level], vec_in.at[level], vec_send.at[level], vec_recv.at[level],
            lax.rem(me + (1 << level), devices),
        )

    last = node3(3)
    for part in range(chunks):
        rows = slice(part * chunk, (part + 1) * chunk)
        first = turned_ref[0, rows], turned_ref[1, rows], turned_ref[2, rows]
        mat_out[0, rows] = matmul(first, last, True)

        @pl.when(sends(0))
        def _():
            mat_copy(0, part).start()

    offset = {steps + t: rep(shift[t : t + 1]) for t in range(steps)}
    for i in range(steps - 1, 0, -1):
        offset[i] = rows_dot(offset[2 * i], node(2 * i + 1)) + offset[2 * i + 1]
    vec_out[0] = offset[1][:1]

    @pl.when(sends(0))
    def _():
        vec_copy(0).start()

    powers = power_hi.shape[0]

    def put_power(k, value):
        power_hi[k], power_lo[k], power_end[k] = split3(value)

    put_power(0, smooth_ref[...])
    for k in range(1, powers):
        base = power_hi[k - 1], power_lo[k - 1], power_end[k - 1]
        put_power(k, matmul(base, base))

    for level in range(levels):
        @pl.when(takes(level))
        def _():
            own = split(mat_out[level])
            for part in range(chunks):
                rows = slice(part * chunk, (part + 1) * chunk)
                mat_copy(level, part).wait_recv()
                arrived = split(mat_in[level, rows])
                left_hi[level, rows], left_lo[level, rows] = arrived
                product = matmul(arrived, own)
                if level + 1 < levels:
                    mat_out[level + 1, rows] = product

                    @pl.when(sends(level + 1))
                    def _():
                        mat_copy(level + 1, part).start()
                else:
                    whole_hi[0, rows], whole_lo[0, rows] = split(product)
            vec_copy(level).wait_recv()
            total = rows_dot(rep(vec_in[level]), own, False) + vec_out[level]
            vec_out[level + 1] = total[:1]
            if level + 1 < levels:
                @pl.when(sends(level + 1))
                def _():
                    vec_copy(level + 1).start()

    ends = lax.rem(me, block) == block - 1
    chain = remote(
        chain_out, chain_in, chain_send, chain_recv, lax.rem(me + block, devices)
    )

    @pl.when(jnp.logical_and(ends, me < block))
    def _():
        state_ref[...] = init_ref[...] / retain

    @pl.when(jnp.logical_and(ends, me >= block))
    def _():
        chain.wait_recv()
        state_ref[...] = chain_in[...]

    @pl.when(jnp.logical_and(ends, me < devices - block))
    def _():
        after = rows_dot(rep(state_ref[...]), (whole_hi[0], whole_lo[0]), False)
        chain_out[...] = after[:1] + vec_out[levels]
        chain.start()

    def down(level, reach):
        return remote(
            down_out.at[level], down_in,
            down_send.at[level, reach], down_recv,
            lax.rem(me + devices + (1 << reach) - (2 << level), devices),
        )

    def gives(level):
        if level == levels - 1:
            return ends
        return takes(level + 1)

    @pl.when(jnp.logical_not(ends))
    def _():
        down(0, 0).wait_recv()
        state_ref[...] = down_in[...]

    for level in range(levels - 1, -1, -1):
        @pl.when(gives(level))
        def _():
            down_out[level] = state_ref[...]
            for reach in range(level, -1, -1):
                down(level, reach).start()

        @pl.when(takes(level))
        def _():
            moved = rows_dot(rep(state_ref[...]), (left_hi[level], left_lo[level]), False)
            state_ref[...] = moved[:1] + vec_in[level]

    state = {1: rep(state_ref[...])}
    for i in range(1, steps):
        state[2 * i] = state[i]
        moved = rows_dot(state[i], node(2 * i))
        state[2 * i + 1] = moved + offset[2 * i]
        if 2 * i >= steps:
            t = 2 * i - steps
            pred_ref[t : t + 1] = moved[:1]
            after = rows_dot(state[2 * i + 1], node(2 * i + 1))
            pred_ref[t + 1 : t + 2] = after[:1]

    pred = pred_ref[...]
    filtered = pred + gain * (obs_ref[...] - pred)
    filtered_ref[...] = filtered
    correction = filtered - pred

    def fold(x, first):
        half = x.shape[0] // 2
        while half >= 1:
            step = power(first + log2(half))
            if half >= 8:
                x = x[:half] + rows_dot(x[half:], step)
            else:
                x = x + rows_dot(pltpu.roll(x, 8 - half, 0), step)
            half //= 2
        return x[:1]

    own_ref[...] = fold(correction, 0)

    def gather_copy(k, device):
        return remote(
            own_ref, gather_ref.at[k - 1], gather_send.at[k - 1], gather_recv.at[k - 1], device
        )

    def give(k, _):
        gather_copy(k, me - k).start()
        return 0

    lax.fori_loop(1, me + 1, give, 0)

    def get(k, _):
        gather_copy(k, lax.rem(me + devices - k, devices)).wait_recv()
        return 0

    lax.fori_loop(1, devices - me, get, 0)
    after = fold(gather_ref[:, 0, :], log2(steps))

    row = lax.broadcasted_iota(jnp.int32, (steps, width), 0)
    entering = rows_dot(rep(after), power(0))
    back = correction + jnp.where(row == steps - 1, entering[:1], 0.0)
    reach = 1
    while reach < steps:
        moved = jnp.where(row < steps - reach, pltpu.roll(back, steps - reach, 0), 0.0)
        back = back + rows_dot(moved, power(log2(reach)))
        reach *= 2
    smoothed_ref[...] = pred + back

    def gave(k, _):
        gather_copy(k, me - k).wait_send()
        return 0

    lax.fori_loop(1, me + 1, gave, 0)

    @pl.when(jnp.logical_and(ends, me < devices - block))
    def _():
        chain.wait_send()

    for level in range(levels):
        @pl.when(sends(level))
        def _():
            for part in range(chunks):
                mat_copy(level, part).wait_send()
            vec_copy(level).wait_send()

        @pl.when(gives(level))
        def _():
            for reach in range(level + 1):
                down(level, reach).wait_send()


def solution(mesh):
    inner, outer = mesh.shape["inner"], mesh.shape["outer"]
    devices = inner * outer
    block = 2 * inner if outer % 2 == 0 else inner
    levels = log2(block)
    chunks = 4

    def shards(jac, obs, gain_filter, gain_smooth, init_mean):
        steps, width = obs.shape
        powers = log2(steps) + log2(devices)
        square = (width, width)
        vec = (1, width)
        dma = pltpu.SemaphoreType.DMA
        return pl.pallas_call(
            functools.partial(kernel, inner, outer, block, chunks),
            out_shape=[jax.ShapeDtypeStruct((steps, width), F32)] * 2,
            in_specs=[pl.BlockSpec(memory_space=pltpu.VMEM)] * 5,
            out_specs=[pl.BlockSpec(memory_space=pltpu.VMEM)] * 2,
            scratch_shapes=[
                pltpu.VMEM((2 * steps, *square), BF16),
                pltpu.VMEM((2 * steps, *square), BF16),
                pltpu.VMEM((2 * steps, *square), BF16),
                pltpu.VMEM((3, *square), BF16),
                pltpu.VMEM((powers, *square), BF16),
                pltpu.VMEM((powers, *square), BF16),
                pltpu.VMEM((powers, *square), BF16),
                pltpu.VMEM((levels, *square), BF16),
                pltpu.VMEM((levels, *square), BF16),
                pltpu.VMEM((1, *square), BF16),
                pltpu.VMEM((1, *square), BF16),
                pltpu.VMEM((levels, *square), F32),
                pltpu.VMEM((levels, *square), F32),
                pltpu.VMEM((levels + 1, *vec), F32),
                pltpu.VMEM((levels, *vec), F32),
                pltpu.VMEM((levels, *vec), F32),
                pltpu.VMEM(vec, F32),
                pltpu.VMEM(vec, F32),
                pltpu.VMEM(vec, F32),
                pltpu.VMEM(vec, F32),
                pltpu.VMEM((steps, width), F32),
                pltpu.VMEM(vec, F32),
                pltpu.VMEM((devices, *vec), F32),
                dma((levels, chunks)), dma((levels, chunks)), dma((levels,)), dma((levels,)),
                dma((levels, levels)), dma, dma, dma,
                dma((devices,)), dma((devices,)),
            ],
            compiler_params=pltpu.CompilerParams(
                collective_id=0, has_side_effects=True, vmem_limit_bytes=48 * 2**20
            ),
        )(jac, obs, gain_filter[None], gain_smooth, init_mean[None])

    return jax.shard_map(
        shards,
        mesh=mesh,
        in_specs=(P(("outer", "inner"), None, None), P(("outer", "inner"), None), P(), P(), P()),
        out_specs=(P(("outer", "inner"), None), P(("outer", "inner"), None)),
        check_vma=False,
    )
```

```python
import functools

import jax
import jax.numpy as jnp
from jax import lax
from jax.experimental import pallas as pl
from jax.experimental.pallas import tpu as pltpu
from jax.sharding import PartitionSpec as P

F32 = jnp.float32
BF16 = jnp.bfloat16
MESH = pl.DeviceIdType.MESH


def log2(count):
    assert count & (count - 1) == 0
    return count.bit_length() - 1


def factors(count):
    found = []
    while count > 1:
        found.append(2)
        count //= found[-1]
    return found


def exponents_of(steps, devices):
    found, unit = [], 1
    for factor in factors(steps) + factors(devices):
        found += [unit * k for k in range(1, factor)]
        unit *= factor
    return found


def split(x):
    high = x.astype(BF16)
    return high, (x - high.astype(F32)).astype(BF16)


def split3(x):
    high = x.astype(BF16)
    rest = x - high.astype(F32)
    middle = rest.astype(BF16)
    return high, middle, (rest - middle.astype(F32)).astype(BF16)


def matmul(a, b, turned=False):
    dims = (((1,), (1 if turned else 0,)), ((), ()))

    def dot(i, j):
        return lax.dot_general(a[i], b[j], dims, preferred_element_type=F32)

    total = dot(0, 1) + dot(1, 0)
    if len(a) == 3:
        total = total + (dot(1, 1) + (dot(0, 2) + dot(2, 0)))
    return dot(0, 0) + total


def rows_dot(x, matrix, turned=True):
    rows = x.shape[0]
    high = x.astype(BF16).astype(F32)
    both = jnp.concatenate([high, x - high], 0).astype(BF16)
    dims = (((1,), (1 if turned else 0,)), ((), ()))
    out = lax.dot_general(both, matrix[0], dims, preferred_element_type=F32)
    out = out + lax.dot_general(both, matrix[1], dims, preferred_element_type=F32)
    return out[:rows] + out[rows:]


def kernel(
    inner, outer, block, chunks,
    jac_hbm, obs_hbm, gain_hbm, smooth_hbm, init_hbm,
    filtered_ref, smoothed_ref,
    jac_ref, obs_ref, gain_ref, smooth_ref, init_ref, jac_sem, arg_sem,
    node_hi, node_lo, node_end, turned_ref, power_hi, power_lo, power_end,
    left_hi, left_lo, whole_hi, whole_lo,
    mat_out, mat_in, vec_out, vec_in, down_out, down_in, chain_out, chain_in,
    state_ref, pred_ref, own_ref, gather_ref,
    mat_send, mat_recv, vec_send, vec_recv, down_send, down_recv,
    chain_send, chain_recv, gather_send, gather_recv,
):
    steps, width = obs_hbm.shape
    devices = inner * outer
    levels = log2(block)
    me = lax.axis_index("outer") * inner + lax.axis_index("inner")

    def place(device):
        return {"outer": lax.div(device, inner), "inner": lax.rem(device, inner)}

    def remote(src, dst, send, recv, device):
        return pltpu.make_async_remote_copy(
            src_ref=src, dst_ref=dst, send_sem=send, recv_sem=recv,
            device_id=place(device), device_id_type=MESH,
        )

    sources = (obs_hbm, gain_hbm, smooth_hbm, init_hbm)
    targets = (obs_ref, gain_ref, smooth_ref, init_ref)
    arg_copies = [
        pltpu.make_async_copy(source, target, arg_sem.at[k])
        for k, (source, target) in enumerate(zip(sources, targets))
    ]
    jac_copies = [
        pltpu.make_async_copy(jac_hbm.at[t], jac_ref.at[t], jac_sem.at[t]) for t in range(steps)
    ]
    for copy in arg_copies[:2] + jac_copies + arg_copies[2:]:
        copy.start()
    gather_ref[...] = jnp.zeros_like(gather_ref)
    barrier = pltpu.get_barrier_semaphore()

    def greet(device):
        pl.semaphore_signal(barrier, inc=1, device_id=place(device), device_id_type=MESH)

    def sends(level):
        span = 2 << level
        return lax.rem(me, span) == span // 2 - 1

    def takes(level):
        span = 2 << level
        return lax.rem(me, span) == span - 1

    for level in range(levels):
        @pl.when(takes(level))
        def _():
            greet(lax.rem(me + devices - (1 << level), devices))

    ends = lax.rem(me, block) == block - 1

    @pl.when(jnp.logical_and(ends, me >= block))
    def _():
        greet(lax.rem(me + devices - block, devices))

    @pl.when(me == devices - 2)
    def _():
        greet(lax.rem(me + 1, devices))

    def rep(row):
        return jnp.broadcast_to(row, (8, width))

    def node(i):
        return node_hi[i], node_lo[i]

    def node3(i):
        return node_hi[i], node_lo[i], node_end[i]

    def put_node(i, value):
        node_hi[i], node_lo[i], node_end[i] = split3(value)

    exponents = exponents_of(steps, devices)

    def power(exponent):
        k = exponents.index(exponent)
        return power_hi[k], power_lo[k]

    def power3(exponent):
        k = exponents.index(exponent)
        return power_hi[k], power_lo[k], power_end[k]

    arg_copies[0].wait()
    arg_copies[1].wait()
    gain = gain_ref[...]
    retain = 1.0 - gain
    shift = obs_ref[...] * (gain / retain)
    group = min(4, steps)
    for start in range(0, steps, group):
        for t in range(start, start + group):
            jac_copies[t].wait()
        for t in range(start, start + group):
            put_node(steps + t, jac_ref[t] * retain)
        for t in range(start, start + group, 2):
            i = (steps + t) // 2
            put_node(i, matmul(node3(2 * i + 1), node3(2 * i)))
    for i in range(steps // 2 - 1, 1, -1):
        put_node(i, matmul(node3(2 * i + 1), node3(2 * i)))
    for copy in arg_copies[2:]:
        copy.wait()
    grid = (width, width)
    eye = lax.broadcasted_iota(jnp.int32, grid, 0) == lax.broadcasted_iota(jnp.int32, grid, 1)
    eye = jnp.where(eye, 1.0, 0.0).astype(BF16)
    for k, piece in enumerate(node3(2)):
        turned = lax.dot_general(eye, piece, (((1,), (1,)), ((), ())), preferred_element_type=F32)
        turned_ref[k] = turned.astype(BF16)

    pl.semaphore_wait(barrier, 1)

    chunk = width // chunks

    def mat_copy(level, part):
        rows = pl.ds(part * chunk, chunk)
        return remote(
            mat_out.at[level, rows], mat_in.at[level, rows],
            mat_send.at[level, part], mat_recv.at[level, part],
            lax.rem(me + (1 << level), devices),
        )

    def vec_copy(level):
        return remote(
            vec_out.at[level], vec_in.at[level], vec_send.at[level], vec_recv.at[level],
            lax.rem(me + (1 << level), devices),
        )

    last = node3(3)
    for part in range(chunks):
        rows = slice(part * chunk, (part + 1) * chunk)
        first = turned_ref[0, rows], turned_ref[1, rows], turned_ref[2, rows]
        mat_out[0, rows] = matmul(first, last, True)

        @pl.when(sends(0))
        def _():
            mat_copy(0, part).start()

    offset = {steps + t: rep(shift[t : t + 1]) for t in range(steps)}
    for i in range(steps - 1, 0, -1):
        offset[i] = rows_dot(offset[2 * i], node(2 * i + 1)) + offset[2 * i + 1]
    vec_out[0] = offset[1][:1]

    @pl.when(sends(0))
    def _():
        vec_copy(0).start()

    def raise_powers(some):
        for exponent in some:
            k = exponents.index(exponent)
            if exponent == 1:
                value = smooth_ref[...]
            elif exponent % 2:
                value = matmul(power3(exponent - 1), power3(1))
            elif exponent // 2 in exponents:
                value = matmul(power3(exponent // 2), power3(exponent // 2))
            else:
                unit = exponents[k - 2]
                value = matmul(power3(exponents[k - 1]), power3(unit))
            power_hi[k], power_lo[k], power_end[k] = split3(value)

    raise_powers([e for e in exponents if e < steps])

    for level in range(levels):
        @pl.when(takes(level))
        def _():
            own = split(mat_out[level])
            for part in range(chunks):
                rows = slice(part * chunk, (part + 1) * chunk)
                mat_copy(level, part).wait_recv()
                arrived = split(mat_in[level, rows])
                left_hi[level, rows], left_lo[level, rows] = arrived
                product = matmul(arrived, own)
                if level + 1 < levels:
                    mat_out[level + 1, rows] = product

                    @pl.when(sends(level + 1))
                    def _():
                        mat_copy(level + 1, part).start()
                else:
                    whole_hi[0, rows], whole_lo[0, rows] = split(product)
            vec_copy(level).wait_recv()
            total = rows_dot(rep(vec_in[level]), own, False) + vec_out[level]
            vec_out[level + 1] = total[:1]
            if level + 1 < levels:
                @pl.when(sends(level + 1))
                def _():
                    vec_copy(level + 1).start()

    chain = remote(
        chain_out, chain_in, chain_send, chain_recv, lax.rem(me + block, devices)
    )

    @pl.when(jnp.logical_and(ends, me < block))
    def _():
        state_ref[...] = init_ref[...] / retain

    @pl.when(jnp.logical_and(ends, me >= block))
    def _():
        chain.wait_recv()
        state_ref[...] = chain_in[...]

    @pl.when(jnp.logical_and(ends, me < devices - block))
    def _():
        after = rows_dot(rep(state_ref[...]), (whole_hi[0], whole_lo[0]), False)
        chain_out[...] = after[:1] + vec_out[levels]
        chain.start()

    def down(level, reach):
        return remote(
            down_out.at[level], down_in,
            down_send.at[level, reach], down_recv,
            lax.rem(me + devices + (1 << reach) - (2 << level), devices),
        )

    def gives(level):
        if level == levels - 1:
            return ends
        return takes(level + 1)

    @pl.when(jnp.logical_not(ends))
    def _():
        down(0, 0).wait_recv()
        state_ref[...] = down_in[...]

    for level in range(levels - 1, -1, -1):
        @pl.when(gives(level))
        def _():
            down_out[level] = state_ref[...]
            for reach in range(level, -1, -1):
                down(level, reach).start()

        @pl.when(takes(level))
        def _():
            moved = rows_dot(rep(state_ref[...]), (left_hi[level], left_lo[level]), False)
            state_ref[...] = moved[:1] + vec_in[level]

    state = {1: rep(state_ref[...])}
    for i in range(1, steps):
        state[2 * i] = state[i]
        moved = rows_dot(state[i], node(2 * i))
        state[2 * i + 1] = moved + offset[2 * i]
        if 2 * i >= steps:
            t = 2 * i - steps
            pred_ref[t : t + 1] = moved[:1]
            after = rows_dot(state[2 * i + 1], node(2 * i + 1))
            pred_ref[t + 1 : t + 2] = after[:1]

    pred = pred_ref[...]
    filtered = pred + gain * (obs_ref[...] - pred)
    filtered_ref[...] = filtered
    correction = filtered - pred

    def fold(x, first):
        half = x.shape[0] // 2
        while half >= 1:
            step = power(first * half)
            if half >= 8:
                x = x[:half] + rows_dot(x[half:], step)
            else:
                x = x + rows_dot(pltpu.roll(x, 8 - half, 0), step)
            half //= 2
        return x[:1]

    own_ref[...] = fold(correction, 1)

    def gather_copy(k, device):
        return remote(
            own_ref, gather_ref.at[k - 1], gather_send.at[k - 1], gather_recv.at[k - 1], device
        )

    def give(device, _):
        gather_copy(me - device, device).start()
        return 0

    lax.fori_loop(0, me, give, 0)
    raise_powers([e for e in exponents if e >= steps])

    def get(k, _):
        gather_copy(k, lax.rem(me + devices - k, devices)).wait_recv()
        return 0

    lax.fori_loop(1, devices - me, get, 0)
    after = fold(gather_ref[:, 0, :], steps)

    row = lax.broadcasted_iota(jnp.int32, (steps, width), 0)
    entering = rows_dot(rep(after), power(1))
    back = correction + jnp.where(row == steps - 1, entering[:1], 0.0)
    reach = 1
    while reach < steps:
        moved = jnp.where(row < steps - reach, pltpu.roll(back, steps - reach, 0), 0.0)
        back = back + rows_dot(moved, power(reach))
        reach *= 2
    smoothed_ref[...] = pred + back

    def gave(k, _):
        gather_copy(k, me - k).wait_send()
        return 0

    lax.fori_loop(1, me + 1, gave, 0)

    @pl.when(jnp.logical_and(ends, me < devices - block))
    def _():
        chain.wait_send()

    for level in range(levels):
        @pl.when(sends(level))
        def _():
            for part in range(chunks):
                mat_copy(level, part).wait_send()
            vec_copy(level).wait_send()

        @pl.when(gives(level))
        def _():
            for reach in range(level + 1):
                down(level, reach).wait_send()


def solution(mesh):
    inner, outer = mesh.shape["inner"], mesh.shape["outer"]
    devices = inner * outer
    block = 2 * inner if outer % 2 == 0 else inner
    levels = log2(block)
    chunks = 4

    def shards(jac, obs, gain_filter, gain_smooth, init_mean):
        steps, width = obs.shape
        powers = len(exponents_of(steps, devices))
        square = (width, width)
        vec = (1, width)
        dma = pltpu.SemaphoreType.DMA
        return pl.pallas_call(
            functools.partial(kernel, inner, outer, block, chunks),
            out_shape=[jax.ShapeDtypeStruct((steps, width), F32)] * 2,
            in_specs=[pl.BlockSpec(memory_space=pl.ANY)] * 5,
            out_specs=[pl.BlockSpec(memory_space=pltpu.VMEM)] * 2,
            scratch_shapes=[
                pltpu.VMEM((steps, *square), F32),
                pltpu.VMEM((steps, width), F32),
                pltpu.VMEM(vec, F32),
                pltpu.VMEM(square, F32),
                pltpu.VMEM(vec, F32),
                dma((steps,)),
                dma((4,)),
                pltpu.VMEM((2 * steps, *square), BF16),
                pltpu.VMEM((2 * steps, *square), BF16),
                pltpu.VMEM((2 * steps, *square), BF16),
                pltpu.VMEM((3, *square), BF16),
                pltpu.VMEM((powers, *square), BF16),
                pltpu.VMEM((powers, *square), BF16),
                pltpu.VMEM((powers, *square), BF16),
                pltpu.VMEM((levels, *square), BF16),
                pltpu.VMEM((levels, *square), BF16),
                pltpu.VMEM((1, *square), BF16),
                pltpu.VMEM((1, *square), BF16),
                pltpu.VMEM((levels, *square), F32),
                pltpu.VMEM((levels, *square), F32),
                pltpu.VMEM((levels + 1, *vec), F32),
                pltpu.VMEM((levels, *vec), F32),
                pltpu.VMEM((levels, *vec), F32),
                pltpu.VMEM(vec, F32),
                pltpu.VMEM(vec, F32),
                pltpu.VMEM(vec, F32),
                pltpu.VMEM(vec, F32),
                pltpu.VMEM((steps, width), F32),
                pltpu.VMEM(vec, F32),
                pltpu.VMEM((devices, *vec), F32),
                dma((levels, chunks)), dma((levels, chunks)), dma((levels,)), dma((levels,)),
                dma((levels, levels)), dma, dma, dma,
                dma((devices,)), dma((devices,)),
            ],
            compiler_params=pltpu.CompilerParams(
                collective_id=0, has_side_effects=True, vmem_limit_bytes=60 * 2**20
            ),
        )(jac, obs, gain_filter[None], gain_smooth, init_mean[None])

    return jax.shard_map(
        shards,
        mesh=mesh,
        in_specs=(P(("outer", "inner"), None, None), P(("outer", "inner"), None), P(), P(), P()),
        out_specs=(P(("outer", "inner"), None), P(("outer", "inner"), None)),
        check_vma=False,
    )
```
